512 devices in a mesh: row: 8 (over y, z_hi), col: 16 (over z_lo, core), depth: 4 (over x).
Axes of the slice: x: 4, y: 4, z: 16 (z_hi: 2, z_lo: 8; z = z_hi * 8 + z_lo), core: 2. Of those that a mesh axis runs over, the one named last changes fastest.
Arguments:
- a_tiles: bfloat16 [8, 16, 4, 4, 128, 128], P('row', 'col', 'depth'), may hold values from -0.625 to 0.625
- pair_lists: int32 [8, 16, 4, 16, 2, 4, 12], P('row', 'col', 'depth'), may hold values from 0 to 31, as said below
Outputs:
- product_blocks: float32 [8, 16, 12, 128, 128], P('row', 'col', 'depth')
The draws below stay inside these ranges and needn't reach their ends.
Inputs may be any that keep to these rules, and one draw needn't show every extreme that they name: pair_lists[..., 0, m, o] is a left slot below 4, or 4 for an empty pair slot; the live pairs of a product block come first; pair_lists[..., 1, m, o] is a slot of the right panel.
All inputs are finite; a program needn't handle non-finite values.
Results may differ from the reference program's by a relative error of at most 0.0003.
Values may be sent and summed in bfloat16 or wider, within the bound.
A program may use at most 64 MiB of HBM per device.

```python
import jax
import jax.numpy as jnp
from jax import lax

BLOCK = 128
S = 4
PAIRS = 4
SHIFTS = 16
RIGHT_SLOTS = 32
OUT_TOT = 12
N_ROW = 8
N_COL = 16
N_DEPTH = 4


def draw_pair_lists(key, part):
    base_key = jax.random.fold_in(key, 7)
    key_count, key_load, key_left, key_right = jax.random.split(base_key, 4)
    head_shape = (N_ROW, N_COL, N_DEPTH, SHIFTS)
    live_count = jax.random.randint(key_count, head_shape + (1, OUT_TOT), 1, PAIRS)
    device_load = jax.random.randint(key_load, (N_ROW, N_COL, N_DEPTH, 1, 1, 1), 0, 2)
    live_count = jnp.minimum(live_count + device_load, PAIRS)
    live_count = live_count.at[:, :, :, :, 0, 0].set(1)
    live_count = live_count.at[:, :, :, :, 0, 1].set(PAIRS)
    position = jnp.arange(PAIRS, dtype=jnp.int32).reshape(PAIRS, 1)
    left_slot = jax.random.randint(key_left, head_shape + (PAIRS, OUT_TOT), 0, S)
    left_slot = jnp.where(position < live_count, left_slot, S)
    right_slot = jax.random.randint(key_right, head_shape + (PAIRS, OUT_TOT), 0, RIGHT_SLOTS)
    right_slot = right_slot.at[:, :, :, 0, 0, 0].set(RIGHT_SLOTS - 1)
    return jnp.stack([left_slot, right_slot], axis=4).astype(jnp.int32)


def levels(stream_key, extent, cuts, least, high):
    loudness, own = 1.0, jax.random.fold_in(stream_key, 6)
    for dim, parts in cuts:
        heights = jnp.exp(jax.random.uniform(jax.random.fold_in(own, dim), (parts,), jnp.float32, least / len(cuts), high / len(cuts)))
        loudness = loudness * jnp.repeat(heights, extent[dim] // parts).reshape([-1 if axis == dim else 1 for axis in range(len(extent))])
    return loudness


def noise(stream_key, dims, width, bound, cuts=(), kind=jnp.bfloat16):
    level = levels(stream_key, dims, cuts, -0.22, 0.18) if cuts else 1.0
    result = jax.random.normal(stream_key, dims, jnp.float32) * width * level
    return jnp.minimum(jnp.maximum(result, -bound), bound).astype(kind)


def setup_inputs(seed: int = 0) -> dict:
    seeds = jax.random.split(jax.random.key(seed), 3)
    return {
        "a_tiles": noise(seeds[0], (N_ROW, N_COL, N_DEPTH, S, BLOCK, BLOCK), 0.1, 0.625, ((0, 8), (1, 16), (2, 4))),
        "pair_lists": draw_pair_lists(jax.random.fold_in(seeds[2], 71), 0),
    }


def reference(a_tiles, pair_lists):
    grid_rows = a_tiles.shape[0]
    grid_cols = a_tiles.shape[1]
    layers = a_tiles.shape[2]
    block_width = a_tiles.shape[4]
    out_total = pair_lists.shape[6]
    zero_block = jnp.zeros((grid_cols, 1, block_width, block_width), a_tiles.dtype)
    shift_index = jnp.arange(grid_cols, dtype=jnp.int32)

    def product_cell(flat_index):
        row_index = flat_index // grid_cols
        col_index = flat_index % grid_cols

        def add_layer(layer_index, running):
            row_tiles = a_tiles[row_index, :, layer_index]
            padded_rows = jnp.concatenate([row_tiles, zero_block], axis=1)
            col_tiles = a_tiles[:, col_index, layer_index].reshape(-1, block_width, block_width)
            pair_table = pair_lists[row_index, col_index, layer_index]
            sources = ((col_index - shift_index) % grid_cols).astype(jnp.int32)
            chosen = padded_rows[sources[:, None, None], pair_table[:, 0]]
            partner = col_tiles[pair_table[:, 1]]
            return running + jnp.einsum("smoik,smojk->oij", chosen.astype(jnp.float32), partner.astype(jnp.float32), precision=lax.Precision.HIGHEST)

        return lax.fori_loop(0, layers, add_layer, jnp.zeros((out_total, block_width, block_width), jnp.float32))

    blocks = lax.map(product_cell, jnp.arange(grid_rows * grid_cols, dtype=jnp.int32))
    return blocks.reshape(grid_rows, grid_cols, out_total, block_width, block_width)
```

```python
import jax
import jax.numpy as jnp
from jax import lax
from jax.experimental import pallas as pl
from jax.experimental.pallas import tpu as pltpu
from jax.sharding import PartitionSpec as P

MESH = pl.DeviceIdType.MESH
LINE = 8
ROWS = 8
COLS = 16
DEPTH = 4
SLOTS = 4
OUTS = 12
SHIFTS = 16
PAIRS = 4
KEEP = OUTS // DEPTH
CHUNKS = 4
PIECE = SLOTS // CHUNKS
RIGHT = COLS
PASSING = COLS + ROWS
POOL = PASSING + 6
SHIFT_STEP = 8
ORDER = (2, 1, 3, 0)


def arrives(place, step):
    return (step <= place) | (step >= place + 5)


def kernel(
    tiles, pairs, out, pool, partial, landed, load_sem, z_send, z_recv, twin_send, twin_recv,
    y_send, y_recv, x_send, x_recv,
):
    row, col, depth = lax.axis_index("row"), lax.axis_index("col"), lax.axis_index("depth")
    spot, core = col // 2, col % 2
    y, group = row // 2, row % 2

    load = [
        pltpu.make_async_copy(tiles, pool.at[col, 0:SLOTS], load_sem.at[0]),
        pltpu.make_async_copy(tiles, pool.at[RIGHT + row, 0:SLOTS], load_sem.at[1]),
    ]
    for copy in load:
        copy.start()

    def beside(sign):
        edge = spot == (LINE - 1 if sign > 0 else 0)
        return {
            "row": jnp.where(edge, row + 1 - 2 * group, row),
            "col": jnp.where(edge, (0 if sign > 0 else LINE - 1) * 2 + core, col + 2 * sign),
        }

    ways = (beside(1), beside(-1))
    twin = {"col": col + 1 - 2 * core}
    y_peer = [{"row": lax.rem(y + k, 4) * 2 + group} for k in (1, 2, 3)]
    x_peer = [{"depth": lax.rem(depth + k, 4)} for k in (1, 2, 3)]

    barrier = pltpu.get_barrier_semaphore()
    peers = [*ways, twin, *y_peer, *x_peer]
    for peer in peers:
        pl.semaphore_signal(barrier, inc=1, device_id=peer, device_id_type=MESH)

    zero = jnp.zeros((128, 128), jnp.bfloat16)
    for k in range(COLS):
        pool[k, SLOTS] = zero
    pl.semaphore_wait(barrier, len(peers))

    place = (spot, LINE - 1 - spot)
    ahead = [lax.rem(p + 1, LINE) for p in place]
    crossing = [p == LINE - 1 for p in place]

    def slot(way, p, r, step):
        source = lax.rem(p - step + LINE, LINE)
        at = source if way == 0 else LINE - 1 - source
        far = RIGHT + r + 1 - 2 * lax.rem(r, 2) if step == LINE else PASSING + way * 3 + (step - 5)
        if step == 0:
            return col
        if step < 5:
            return at * 2 + core
        return jnp.where(step <= p, at * 2 + core, far)

    def z_copy(way, step, piece):
        theirs = jnp.where(crossing[way], row + 1 - 2 * group, row)
        part = pl.ds(piece * PIECE, PIECE)
        return pltpu.make_async_remote_copy(
            src_ref=pool.at[slot(way, place[way], row, step - 1), part],
            dst_ref=pool.at[slot(way, ahead[way], theirs, step), part],
            send_sem=z_send.at[way, step - 1, piece],
            recv_sem=z_recv.at[way, step - 1, piece],
            device_id=ways[way],
            device_id_type=MESH,
        )

    def z_wait(way, step, piece):
        part = pl.ds(piece * PIECE, PIECE)
        here = pool.at[slot(way, place[way], row, step), part]
        pltpu.make_async_remote_copy(
            src_ref=here, dst_ref=here, send_sem=z_send.at[way, step - 1, piece],
            recv_sem=z_recv.at[way, step - 1, piece], device_id=ways[way], device_id_type=MESH,
        ).wait_recv()

    def twin_copy(at):
        ref = pool.at[at * 2 + core, 0:SLOTS]
        return pltpu.make_async_remote_copy(
            src_ref=ref, dst_ref=ref, send_sem=twin_send.at[at], recv_sem=twin_recv.at[at],
            device_id=twin, device_id_type=MESH,
        )

    def twin_wait(at):
        ref = pool.at[at * 2 + 1 - core, 0:SLOTS]
        pltpu.make_async_remote_copy(
            src_ref=ref, dst_ref=ref, send_sem=twin_send.at[at], recv_sem=twin_recv.at[at],
            device_id=twin, device_id_type=MESH,
        ).wait_recv()

    def y_copy(kind, k):
        ref = pool.at[RIGHT + (row if kind == 0 else row + 1 - 2 * group), 0:SLOTS]
        return pltpu.make_async_remote_copy(
            src_ref=ref, dst_ref=ref, send_sem=y_send.at[kind, k], recv_sem=y_recv.at[kind, k],
            device_id=y_peer[k], device_id_type=MESH,
        )

    def y_wait(kind, k):
        source = lax.rem(y + 3 - k, 4) * 2 + (group if kind == 0 else 1 - group)
        ref = pool.at[RIGHT + source, 0:SLOTS]
        pltpu.make_async_remote_copy(
            src_ref=ref, dst_ref=ref, send_sem=y_send.at[kind, k], recv_sem=y_recv.at[kind, k],
            device_id=y_peer[k], device_id_type=MESH,
        ).wait_recv()

    for copy in load:
        copy.wait()
    for piece in range(CHUNKS):
        for way in range(2):
            @pl.when(arrives(ahead[way], 1))
            def _():
                z_copy(way, 1, piece).start()
    twin_copy(spot).start()
    for k in range(3):
        y_copy(0, k).start()

    for step in range(1, LINE + 1):
        for piece in range(CHUNKS):
            for way in range(2):
                @pl.when(arrives(place[way], step))
                def _():
                    z_wait(way, step, piece)
                    if step < LINE:
                        @pl.when(arrives(ahead[way], step + 1))
                        def _():
                            z_copy(way, step + 1, piece).start()
                    if piece == CHUNKS - 1:
                        if step < LINE:
                            @pl.when(step <= place[way])
                            def _():
                                twin_copy(spot - step if way == 0 else spot + step).start()
                        else:
                            for k in range(3):
                                y_copy(1, k).start()

    for at in range(LINE):
        twin_wait(at)
    for kind in range(2):
        for k in range(3):
            y_wait(kind, k)

    def block(o):
        def some(group_of, total):
            lefts, rights = [], []
            for inner in range(SHIFT_STEP):
                shift = group_of * SHIFT_STEP + inner
                source = lax.rem(col - shift + COLS, COLS)
                for m in range(PAIRS):
                    lefts.append(pool[source, pairs[0, o, m, shift]])
                    pick = pairs[1, o, m, shift]
                    rights.append(pool[RIGHT + pick // SLOTS, lax.rem(pick, SLOTS)])
            return total + lax.dot_general(
                jnp.concatenate(lefts, axis=1), jnp.concatenate(rights, axis=1),
                (((1,), (1,)), ((), ())), preferred_element_type=jnp.float32,
            )

        return lax.fori_loop(0, SHIFTS // SHIFT_STEP, some, jnp.zeros((128, 128), jnp.float32))

    def x_copy(k, i):
        return pltpu.make_async_remote_copy(
            src_ref=partial.at[k - 1, i], dst_ref=landed.at[k - 1, i],
            send_sem=x_send.at[k - 1, i], recv_sem=x_recv.at[k - 1, i],
            device_id=x_peer[k - 1], device_id_type=MESH,
        )

    for k in ORDER:
        owner = lax.rem(depth + k, DEPTH)

        def one(i, _):
            value = block(owner * KEEP + i)
            if k:
                partial[k - 1, i] = value
                x_copy(k, i).start()
            else:
                out[i] = value
            return 0

        lax.fori_loop(0, KEEP, one, 0)

    for k in ORDER[:-1]:
        for i in range(KEEP):
            x_copy(k, i).wait_recv()
    for i in range(KEEP):
        out[i] = out[i] + landed[0, i] + landed[1, i] + landed[2, i]

    for k in ORDER[:-1]:
        for i in range(KEEP):
            x_copy(k, i).wait_send()
    for step in range(1, LINE + 1):
        for way in range(2):
            @pl.when(arrives(ahead[way], step))
            def _():
                for piece in range(CHUNKS):
                    z_copy(way, step, piece).wait_send()
    for at in range(LINE):
        twin_copy(at).wait_send()
    for kind in range(2):
        for k in range(3):
            y_copy(kind, k).wait_send()


def body(a_tiles, pair_lists):
    tiles = a_tiles.reshape(a_tiles.shape[3:])
    pairs = jnp.transpose(pair_lists.reshape(pair_lists.shape[3:]), (1, 3, 2, 0))
    reduced = pl.pallas_call(
        kernel,
        out_shape=jax.ShapeDtypeStruct((KEEP, 128, 128), jnp.float32),
        in_specs=[
            pl.BlockSpec(memory_space=pl.ANY),
            pl.BlockSpec(memory_space=pltpu.SMEM),
        ],
        out_specs=pl.BlockSpec(memory_space=pltpu.VMEM),
        scratch_shapes=[
            pltpu.VMEM((POOL, SLOTS + 1, 128, 128), jnp.bfloat16),
            pltpu.VMEM((DEPTH - 1, KEEP, 128, 128), jnp.float32),
            pltpu.VMEM((DEPTH - 1, KEEP, 128, 128), jnp.float32),
            pltpu.SemaphoreType.DMA((2,)),
            pltpu.SemaphoreType.DMA((2, LINE, CHUNKS)),
            pltpu.SemaphoreType.DMA((2, LINE, CHUNKS)),
            pltpu.SemaphoreType.DMA((LINE,)),
            pltpu.SemaphoreType.DMA((LINE,)),
            pltpu.SemaphoreType.DMA((2, 3)),
            pltpu.SemaphoreType.DMA((2, 3)),
            pltpu.SemaphoreType.DMA((DEPTH - 1, KEEP)),
            pltpu.SemaphoreType.DMA((DEPTH - 1, KEEP)),
        ],
        compiler_params=pltpu.CompilerParams(
            collective_id=0, has_side_effects=True, vmem_limit_bytes=16 << 20
        ),
        name="cannon",
    )(tiles, pairs)
    return reduced.reshape((1, 1) + reduced.shape)


def solution(mesh):
    placed = (
        P("row", "col", "depth", None, None, None),
        P("row", "col", "depth", None, None, None, None),
    )
    return jax.shard_map(
        body,
        mesh=mesh,
        in_specs=placed,
        out_specs=P("row", "col", "depth", None, None),
        check_vma=False,
    )
```

```python
import jax
import jax.numpy as jnp
from jax import lax
from jax.experimental import pallas as pl
from jax.experimental.pallas import tpu as pltpu
from jax.sharding import PartitionSpec as P

MESH = pl.DeviceIdType.MESH
LINE = 8
ROWS = 8
COLS = 16
DEPTH = 4
SLOTS = 4
OUTS = 12
SHIFTS = 16
PAIRS = 4
KEEP = OUTS // DEPTH
CHUNKS = 4
PIECE = SLOTS // CHUNKS
RIGHT = COLS
POOL = COLS + ROWS
HALF = LINE // 2
FAR_STEP = 5
SHIFT_STEP = 16
ORDER = (2, 1, 3, 0)


def remote(src, dst, send, recv, device):
    return pltpu.make_async_remote_copy(
        src_ref=src, dst_ref=dst, send_sem=send, recv_sem=recv, device_id=device, device_id_type=MESH
    )


def kernel(
    tiles, pair_table, out, pool, pairs, partial, landed, load_sem, z_send, z_recv, twin_send,
    twin_recv, far_send, far_recv, far_ready, y_send, y_recv, x_send, x_recv,
):
    row, col, depth = lax.axis_index("row"), lax.axis_index("col"), lax.axis_index("depth")
    spot, core = col // 2, col % 2
    y, group = row // 2, row % 2
    other = row + 1 - 2 * group

    load = [
        pltpu.make_async_copy(tiles, pool.at[col, 0:SLOTS], load_sem.at[0]),
        pltpu.make_async_copy(tiles, pool.at[RIGHT + row, 0:SLOTS], load_sem.at[1]),
        pltpu.make_async_copy(pair_table, pairs, load_sem.at[2]),
    ]
    for copy in load:
        copy.start()

    sign = 1 - 2 * core
    place = core * (LINE - 1) + sign * spot
    first, last = place == 0, place == LINE - 1
    after = {"col": col + jnp.where(last, -(LINE - 1), 1) * sign * 2}
    before = {"col": col + jnp.where(first, LINE - 1, -1) * sign * 2}
    twin = {"col": col + sign}
    y_peer = [{"row": lax.rem(y + k, 4) * 2 + group} for k in (1, 2, 3)]
    x_peer = [{"depth": lax.rem(depth + k, 4)} for k in (1, 2, 3)]

    def far_peer(source, plane):
        return {"row": other, "col": (core * (LINE - 1) + sign * source) * 2 + plane}

    relay = {"row": other, "col": jnp.where(spot >= HALF, 1, COLS - 2)}
    partner = {"row": other}
    low = group == 0
    relays = low & last

    barrier = pltpu.get_barrier_semaphore()

    def greet(device):
        pl.semaphore_signal(barrier, inc=1, device_id=device, device_id_type=MESH)

    around = [twin, *y_peer, *x_peer]
    for peer in around:
        greet(peer)

    @pl.when(place > 0)
    def _():
        greet(before)

    @pl.when(low)
    def _():
        greet(partner)

    @pl.when(relays)
    def _():
        for source in range(HALF):
            for plane in range(2):
                greet(far_peer(source, plane))

    pl.semaphore_wait(barrier, len(around) + jnp.where(last, 0, 1) + 2 * group)

    @pl.when(group == 1)
    def _():
        pl.semaphore_signal(far_ready, inc=1, device_id=relay, device_id_type=MESH)

    def at(chip):
        return (core * (LINE - 1) + sign * chip) * 2

    def plane_of(turn):
        return core if turn == 0 else 1 - core

    def z_copy(step, turn, piece):
        ref = pool.at[at(place - step + 1) + plane_of(turn), pl.ds(piece * PIECE, PIECE)]
        return remote(
            ref, ref, z_send.at[step - 1, turn, piece], z_recv.at[step - 1, turn, piece], after
        )

    def z_wait(step, turn, piece):
        here = pool.at[at(place - step) + plane_of(turn), pl.ds(piece * PIECE, PIECE)]
        remote(here, here, z_send.at[step - 1, turn, piece], z_recv.at[step - 1, turn, piece], after).wait_recv()

    def twin_copy(step):
        ref = pool.at[pl.ds((core * (LINE - 1) + sign * (place - step)) * 2, 2), 0:SLOTS]
        return remote(ref, ref, twin_send.at[step], twin_recv.at[step], twin)

    def twin_wait(step):
        ref = pool.at[pl.ds((core * (LINE - 1) + sign * (place + step)) * 2, 2), 0:SLOTS]
        remote(ref, ref, twin_send.at[step], twin_recv.at[step], twin).wait_recv()

    own_copy = remote(
        pool.at[col, 0:SLOTS], pool.at[col, 0:SLOTS], twin_send.at[0], twin_recv.at[0], twin
    )
    twins = pool.at[col + sign, 0:SLOTS]
    own_wait = remote(twins, twins, twin_send.at[0], twin_recv.at[0], twin)

    def far_copy(step, turn, piece):
        part = pl.ds(piece * PIECE, PIECE)
        return remote(
            pool.at[at(place - step) + plane_of(turn), part], pool.at[RIGHT + row, part],
            far_send.at[step - HALF, turn, piece], far_recv.at[piece], far_peer(place - step, plane_of(turn)),
        )

    def direct_copy(piece):
        part = pl.ds(piece * PIECE, PIECE)
        return remote(
            pool.at[col, part], pool.at[RIGHT + row, part], far_send.at[0, 0, piece], far_recv.at[piece], partner
        )

    def pass_far():
        for piece in range(CHUNKS):
            here = pool.at[RIGHT + other, pl.ds(piece * PIECE, PIECE)]
            remote(here, here, far_send.at[0, 0, piece], far_recv.at[piece], partner).wait_recv()
            for k in range(3):
                y_copy(1 + piece, k).start()

    def y_copy(kind, k):
        part = pl.ds((kind - 1) * PIECE, PIECE) if kind else slice(0, SLOTS)
        ref = pool.at[RIGHT + (other if kind else row), part]
        return remote(ref, ref, y_send.at[kind, k], y_recv.at[kind, k], y_peer[k])

    def y_wait(kind, k):
        source = lax.rem(y + 3 - k, 4) * 2 + (1 - group if kind else group)
        part = pl.ds((kind - 1) * PIECE, PIECE) if kind else slice(0, SLOTS)
        ref = pool.at[RIGHT + source, part]
        remote(ref, ref, y_send.at[kind, k], y_recv.at[kind, k], y_peer[k]).wait_recv()

    load[0].wait()
    own_copy.start()

    @pl.when(group == 1)
    def _():
        for piece in range(CHUNKS):
            direct_copy(piece).start()

    @pl.when(place < LINE - 1)
    def _():
        for piece in range(CHUNKS):
            z_copy(1, 0, piece).start()

    load[1].wait()
    for k in range(3):
        y_copy(0, k).start()
    own_wait.wait_recv()

    @pl.when(place < LINE - 1)
    def _():
        for piece in range(CHUNKS):
            z_copy(1, 1, piece).start()

    zero = jnp.zeros((128, 128), jnp.bfloat16)
    for k in range(COLS):
        pool[k, SLOTS] = zero

    for step in range(1, LINE):
        @pl.when(step <= place)
        def _():
            if step == HALF:
                @pl.when(relays)
                def _():
                    pl.semaphore_wait(far_ready, 2 * HALF)

            for turn in range(2):
                for piece in range(CHUNKS):
                    z_wait(step, turn, piece)

                    @pl.when(place < LINE - 1)
                    def _():
                        z_copy(step + 1, turn, piece).start()

                    if step >= HALF:
                        @pl.when(relays)
                        def _():
                            far_copy(step, turn, piece).start()
            twin_copy(step).start()
            if step == FAR_STEP:
                pass_far()

    @pl.when(place < FAR_STEP)
    def _():
        pass_far()

    for step in range(1, LINE):
        @pl.when(place + step < LINE)
        def _():
            twin_wait(step)

    load[2].wait()
    for kind in range(1 + CHUNKS):
        for k in range(3):
            y_wait(kind, k)

    def block(o):
        def some(group_of, total):
            lefts, rights = [], []
            for inner in range(SHIFT_STEP):
                shift = group_of * SHIFT_STEP + inner
                source = lax.rem(col - shift + COLS, COLS)
                for m in range(PAIRS):
                    lefts.append(pool[source, pairs[0, o, m, shift]])
                    pick = pairs[1, o, m, shift]
                    rights.append(pool[RIGHT + pick // SLOTS, lax.rem(pick, SLOTS)])
            value = lax.dot_general(
                jnp.concatenate(lefts, axis=1), jnp.concatenate(rights, axis=1),
                (((1,), (1,)), ((), ())), preferred_element_type=jnp.float32,
            )
            return value if total is None else total + value

        if SHIFT_STEP == SHIFTS:
            return some(0, None)
        return lax.fori_loop(0, SHIFTS // SHIFT_STEP, some, jnp.zeros((128, 128), jnp.float32))

    def x_copy(k, i):
        return remote(
            partial.at[k - 1, i], landed.at[k - 1, i], x_send.at[k - 1, i], x_recv.at[k - 1, i], x_peer[k - 1]
        )

    for k in ORDER:
        owner = lax.rem(depth + k, DEPTH)

        def one(i, _):
            value = block(owner * KEEP + i)
            if k:
                partial[k - 1, i] = value
                x_copy(k, i).start()
            else:
                out[i] = value
            return 0

        lax.fori_loop(0, KEEP, one, 0)

    for k in ORDER[:-1]:
        for i in range(KEEP):
            x_copy(k, i).wait_recv()
    for i in range(KEEP):
        out[i] = out[i] + landed[0, i] + landed[1, i] + landed[2, i]

    for k in ORDER[:-1]:
        for i in range(KEEP):
            x_copy(k, i).wait_send()
    @pl.when(place < LINE - 1)
    def _():
        for step in range(1, LINE):
            @pl.when(step <= place + 1)
            def _():
                for turn in range(2):
                    for piece in range(CHUNKS):
                        z_copy(step, turn, piece).wait_send()

    @pl.when(group == 1)
    def _():
        for piece in range(CHUNKS):
            direct_copy(piece).wait_send()

    @pl.when(relays)
    def _():
        for step in range(HALF, LINE):
            for turn in range(2):
                for piece in range(CHUNKS):
                    far_copy(step, turn, piece).wait_send()

    own_copy.wait_send()
    for step in range(1, LINE):
        @pl.when(step <= place)
        def _():
            twin_copy(step).wait_send()
    for kind in range(1 + CHUNKS):
        for k in range(3):
            y_copy(kind, k).wait_send()


def body(a_tiles, pair_lists):
    tiles = a_tiles.reshape(a_tiles.shape[3:])
    pairs = jnp.transpose(pair_lists.reshape(pair_lists.shape[3:]), (1, 3, 2, 0))
    reduced = pl.pallas_call(
        kernel,
        out_shape=jax.ShapeDtypeStruct((KEEP, 128, 128), jnp.float32),
        in_specs=[
            pl.BlockSpec(memory_space=pltpu.HBM),
            pl.BlockSpec(memory_space=pltpu.HBM),
        ],
        out_specs=pl.BlockSpec(memory_space=pltpu.VMEM),
        scratch_shapes=[
            pltpu.VMEM((POOL, SLOTS + 1, 128, 128), jnp.bfloat16),
            pltpu.SMEM((2, OUTS, PAIRS, SHIFTS), jnp.int32),
            pltpu.VMEM((DEPTH - 1, KEEP, 128, 128), jnp.float32),
            pltpu.VMEM((DEPTH - 1, KEEP, 128, 128), jnp.float32),
            pltpu.SemaphoreType.DMA((3,)),
            pltpu.SemaphoreType.DMA((LINE - 1, 2, CHUNKS)),
            pltpu.SemaphoreType.DMA((LINE - 1, 2, CHUNKS)),
            pltpu.SemaphoreType.DMA((LINE,)),
            pltpu.SemaphoreType.DMA((LINE,)),
            pltpu.SemaphoreType.DMA((LINE - HALF, 2, CHUNKS)),
            pltpu.SemaphoreType.DMA((CHUNKS,)),
            pltpu.SemaphoreType.REGULAR,
            pltpu.SemaphoreType.DMA((1 + CHUNKS, 3)),
            pltpu.SemaphoreType.DMA((1 + CHUNKS, 3)),
            pltpu.SemaphoreType.DMA((DEPTH - 1, KEEP)),
            pltpu.SemaphoreType.DMA((DEPTH - 1, KEEP)),
        ],
        compiler_params=pltpu.CompilerParams(
            collective_id=0, has_side_effects=True, vmem_limit_bytes=60 << 20
        ),
        name="cannon",
    )(tiles, pairs)
    return reduced.reshape((1, 1) + reduced.shape)


def solution(mesh):
    placed = (
        P("row", "col", "depth", None, None, None),
        P("row", "col", "depth", None, None, None, None),
    )
    return jax.shard_map(
        body,
        mesh=mesh,
        in_specs=placed,
        out_specs=P("row", "col", "depth", None, None),
        check_vma=False,
    )
```

```python
import jax
import jax.numpy as jnp
from jax import lax
from jax.experimental import pallas as pl
from jax.experimental.pallas import tpu as pltpu
from jax.sharding import PartitionSpec as P

MESH = pl.DeviceIdType.MESH
LINE = 8
ROWS = 8
COLS = 16
DEPTH = 4
SLOTS = 4
OUTS = 12
SHIFTS = 16
PAIRS = 4
KEEP = OUTS // DEPTH
CHUNKS = 4
PIECE = SLOTS // CHUNKS
RIGHT = COLS
POOL = COLS + ROWS
HALF = LINE // 2
FAR_STEP = 5
SHIFT_STEP = 16
ORDER = (2, 1, 3, 0)


def remote(src, dst, send, recv, device):
    return pltpu.make_async_remote_copy(
        src_ref=src, dst_ref=dst, send_sem=send, recv_sem=recv, device_id=device, device_id_type=MESH
    )


def kernel(
    tiles, pair_table, out, pool, pairs, partial, landed, load_sem, z_send, z_recv, twin_send,
    twin_recv, far_send, far_recv, far_ready, y_send, y_recv, x_send, x_recv,
):
    row, col, depth = lax.axis_index("row"), lax.axis_index("col"), lax.axis_index("depth")
    spot, core = col // 2, col % 2
    y, group = row // 2, row % 2
    other = row + 1 - 2 * group

    load = [
        pltpu.make_async_copy(tiles, pool.at[col, 0:SLOTS], load_sem.at[0]),
        pltpu.make_async_copy(tiles, pool.at[RIGHT + row, 0:SLOTS], load_sem.at[1]),
        pltpu.make_async_copy(pair_table, pairs, load_sem.at[2]),
    ]
    for copy in load:
        copy.start()

    sign = 1 - 2 * core
    place = core * (LINE - 1) + sign * spot
    first, last = place == 0, place == LINE - 1
    after = {"col": col + jnp.where(last, -(LINE - 1), 1) * sign * 2}
    before = {"col": col + jnp.where(first, LINE - 1, -1) * sign * 2}
    twin = {"col": col + sign}
    y_peer = [{"row": lax.rem(y + k, 4) * 2 + group} for k in (1, 2, 3)]
    x_peer = [{"depth": lax.rem(depth + k, 4)} for k in (1, 2, 3)]

    def far_peer(source, plane):
        return {"row": other, "col": (core * (LINE - 1) + sign * source) * 2 + plane}

    relay = {"row": other, "col": jnp.where(spot >= HALF, 1, COLS - 2)}
    partner = {"row": other}
    low = group == 0
    relays = low & last

    barrier = pltpu.get_barrier_semaphore()

    def greet(device):
        pl.semaphore_signal(barrier, inc=1, device_id=device, device_id_type=MESH)

    around = [twin, *y_peer, *x_peer]
    for peer in around:
        greet(peer)

    @pl.when(place > 0)
    def _():
        greet(before)

    @pl.when(low)
    def _():
        greet(partner)

    @pl.when(relays)
    def _():
        for source in range(HALF):
            for plane in range(2):
                greet(far_peer(source, plane))

    pl.semaphore_wait(barrier, len(around) + jnp.where(last, 0, 1) + 2 * group)

    @pl.when(group == 1)
    def _():
        pl.semaphore_signal(far_ready, inc=1, device_id=relay, device_id_type=MESH)

    def at(chip):
        return (core * (LINE - 1) + sign * chip) * 2

    def plane_of(turn):
        return core if turn == 0 else 1 - core

    def z_copy(step, turn, piece):
        ref = pool.at[at(place - step + 1) + plane_of(turn), pl.ds(piece * PIECE, PIECE)]
        return remote(
            ref, ref, z_send.at[step - 1, turn, piece], z_recv.at[step - 1, turn, piece], after
        )

    def z_wait(step, turn, piece):
        here = pool.at[at(place - step) + plane_of(turn), pl.ds(piece * PIECE, PIECE)]
        remote(here, here, z_send.at[step - 1, turn, piece], z_recv.at[step - 1, turn, piece], after).wait_recv()

    def twin_copy(step):
        ref = pool.at[pl.ds((core * (LINE - 1) + sign * (place - step)) * 2, 2), 0:SLOTS]
        return remote(ref, ref, twin_send.at[step], twin_recv.at[step], twin)

    def twin_wait(step):
        ref = pool.at[pl.ds((core * (LINE - 1) + sign * (place + step)) * 2, 2), 0:SLOTS]
        remote(ref, ref, twin_send.at[step], twin_recv.at[step], twin).wait_recv()

    own_copy = remote(
        pool.at[col, 0:SLOTS], pool.at[col, 0:SLOTS], twin_send.at[0], twin_recv.at[0], twin
    )
    twins = pool.at[col + sign, 0:SLOTS]
    own_wait = remote(twins, twins, twin_send.at[0], twin_recv.at[0], twin)

    def far_copy(step, turn, piece):
        part = pl.ds(piece * PIECE, PIECE)
        return remote(
            pool.at[at(place - step) + plane_of(turn), part], pool.at[RIGHT + row, part],
            far_send.at[step - HALF, turn, piece], far_recv.at[piece], far_peer(place - step, plane_of(turn)),
        )

    def direct_copy(piece):
        part = pl.ds(piece * PIECE, PIECE)
        return remote(
            pool.at[col, part], pool.at[RIGHT + row, part], far_send.at[0, 0, piece], far_recv.at[piece], partner
        )

    def pass_far():
        for piece in range(CHUNKS):
            here = pool.at[RIGHT + other, pl.ds(piece * PIECE, PIECE)]
            remote(here, here, far_send.at[0, 0, piece], far_recv.at[piece], partner).wait_recv()
            for k in range(3):
                y_copy(1 + piece, k).start()

    def y_copy(kind, k):
        part = pl.ds((kind - 1) * PIECE, PIECE) if kind else slice(0, SLOTS)
        ref = pool.at[RIGHT + (other if kind else row), part]
        return remote(ref, ref, y_send.at[kind, k], y_recv.at[kind, k], y_peer[k])

    def y_wait(kind, k):
        source = lax.rem(y + 3 - k, 4) * 2 + (1 - group if kind else group)
        part = pl.ds((kind - 1) * PIECE, PIECE) if kind else slice(0, SLOTS)
        ref = pool.at[RIGHT + source, part]
        remote(ref, ref, y_send.at[kind, k], y_recv.at[kind, k], y_peer[k]).wait_recv()

    load[0].wait()
    own_copy.start()

    @pl.when(place < LINE - 1)
    def _():
        for piece in range(CHUNKS):
            z_copy(1, 0, piece).start()

    load[1].wait()
    for k in range(3):
        y_copy(0, k).start()
    own_wait.wait_recv()

    @pl.when(place < LINE - 1)
    def _():
        for piece in range(CHUNKS):
            z_copy(1, 1, piece).start()

    @pl.when(group == 1)
    def _():
        for piece in range(CHUNKS):
            direct_copy(piece).start()

    zero = jnp.zeros((128, 128), jnp.bfloat16)
    for k in range(COLS):
        pool[k, SLOTS] = zero

    for step in range(1, LINE):
        @pl.when(step <= place)
        def _():
            if step == HALF:
                @pl.when(relays)
                def _():
                    pl.semaphore_wait(far_ready, 2 * HALF)

            for turn in range(2):
                for piece in range(CHUNKS):
                    z_wait(step, turn, piece)

                    @pl.when(place < LINE - 1)
                    def _():
                        z_copy(step + 1, turn, piece).start()

                    if step >= HALF:
                        @pl.when(relays)
                        def _():
                            far_copy(step, turn, piece).start()
            twin_copy(step).start()
            if step == FAR_STEP:
                pass_far()

    @pl.when(place < FAR_STEP)
    def _():
        pass_far()

    for step in range(1, LINE):
        @pl.when(place + step < LINE)
        def _():
            twin_wait(step)

    load[2].wait()
    for kind in range(1 + CHUNKS):
        for k in range(3):
            y_wait(kind, k)

    def block(o):
        def some(group_of, total):
            lefts, rights = [], []
            for inner in range(SHIFT_STEP):
                shift = group_of * SHIFT_STEP + inner
                source = lax.rem(col - shift + COLS, COLS)
                for m in range(PAIRS):
                    lefts.append(pool[source, pairs[0, o, m, shift]])
                    pick = pairs[1, o, m, shift]
                    rights.append(pool[RIGHT + pick // SLOTS, lax.rem(pick, SLOTS)])
            value = lax.dot_general(
                jnp.concatenate(lefts, axis=1), jnp.concatenate(rights, axis=1),
                (((1,), (1,)), ((), ())), preferred_element_type=jnp.float32,
            )
            return value if total is None else total + value

        if SHIFT_STEP == SHIFTS:
            return some(0, None)
        return lax.fori_loop(0, SHIFTS // SHIFT_STEP, some, jnp.zeros((128, 128), jnp.float32))

    def x_copy(k, i):
        return remote(
            partial.at[k - 1, i], landed.at[k - 1, i], x_send.at[k - 1, i], x_recv.at[k - 1, i], x_peer[k - 1]
        )

    for k in ORDER:
        owner = lax.rem(depth + k, DEPTH)

        def one(i, _):
            value = block(owner * KEEP + i)
            if k:
                partial[k - 1, i] = value
                x_copy(k, i).start()
            else:
                out[i] = value
            return 0

        lax.fori_loop(0, KEEP, one, 0)

    for k in ORDER[:-1]:
        for i in range(KEEP):
            x_copy(k, i).wait_recv()
    for i in range(KEEP):
        out[i] = out[i] + landed[0, i] + landed[1, i] + landed[2, i]

    for k in ORDER[:-1]:
        for i in range(KEEP):
            x_copy(k, i).wait_send()
    @pl.when(place < LINE - 1)
    def _():
        for step in range(1, LINE):
            @pl.when(step <= place + 1)
            def _():
                for turn in range(2):
                    for piece in range(CHUNKS):
                        z_copy(step, turn, piece).wait_send()

    @pl.when(group == 1)
    def _():
        for piece in range(CHUNKS):
            direct_copy(piece).wait_send()

    @pl.when(relays)
    def _():
        for step in range(HALF, LINE):
            for turn in range(2):
                for piece in range(CHUNKS):
                    far_copy(step, turn, piece).wait_send()

    own_copy.wait_send()
    for step in range(1, LINE):
        @pl.when(step <= place)
        def _():
            twin_copy(step).wait_send()
    for kind in range(1 + CHUNKS):
        for k in range(3):
            y_copy(kind, k).wait_send()


def body(a_tiles, pair_lists):
    tiles = a_tiles.reshape(a_tiles.shape[3:])
    pairs = jnp.transpose(pair_lists.reshape(pair_lists.shape[3:]), (1, 3, 2, 0))
    reduced = pl.pallas_call(
        kernel,
        out_shape=jax.ShapeDtypeStruct((KEEP, 128, 128), jnp.float32),
        in_specs=[
            pl.BlockSpec(memory_space=pltpu.HBM),
            pl.BlockSpec(memory_space=pltpu.HBM),
        ],
        out_specs=pl.BlockSpec(memory_space=pltpu.VMEM),
        scratch_shapes=[
            pltpu.VMEM((POOL, SLOTS + 1, 128, 128), jnp.bfloat16),
            pltpu.SMEM((2, OUTS, PAIRS, SHIFTS), jnp.int32),
            pltpu.VMEM((DEPTH - 1, KEEP, 128, 128), jnp.float32),
            pltpu.VMEM((DEPTH - 1, KEEP, 128, 128), jnp.float32),
            pltpu.SemaphoreType.DMA((3,)),
            pltpu.SemaphoreType.DMA((LINE - 1, 2, CHUNKS)),
            pltpu.SemaphoreType.DMA((LINE - 1, 2, CHUNKS)),
            pltpu.SemaphoreType.DMA((LINE,)),
            pltpu.SemaphoreType.DMA((LINE,)),
            pltpu.SemaphoreType.DMA((LINE - HALF, 2, CHUNKS)),
            pltpu.SemaphoreType.DMA((CHUNKS,)),
            pltpu.SemaphoreType.REGULAR,
            pltpu.SemaphoreType.DMA((1 + CHUNKS, 3)),
            pltpu.SemaphoreType.DMA((1 + CHUNKS, 3)),
            pltpu.SemaphoreType.DMA((DEPTH - 1, KEEP)),
            pltpu.SemaphoreType.DMA((DEPTH - 1, KEEP)),
        ],
        compiler_params=pltpu.CompilerParams(
            collective_id=0, has_side_effects=True, vmem_limit_bytes=60 << 20
        ),
        name="cannon",
    )(tiles, pairs)
    return reduced.reshape((1, 1) + reduced.shape)


def solution(mesh):
    placed = (
        P("row", "col", "depth", None, None, None),
        P("row", "col", "depth", None, None, None, None),
    )
    return jax.shard_map(
        body,
        mesh=mesh,
        in_specs=placed,
        out_specs=P("row", "col", "depth", None, None),
        check_vma=False,
    )
```
